32 devices in a mesh: seq: 4 (over z), dp: 8 (over y, x, core).
Axes of the slice: x: 2, y: 2, z: 4, core: 2. Of those that a mesh axis runs over, the one named last changes fastest.
Arguments:
- qkv: bfloat16 [8, 3, 512, 16, 128], P('dp', None, 'seq'), may hold values from -14 to 14
- cotangent: bfloat16 [8, 512, 3072], P('dp', 'seq'), may hold values from -6 to 6
- w_proj: bfloat16 [2048, 3072], replicated, may hold values from -0.125 to 0.125
- clip_levels: float32 [3072], replicated, may hold values from 0.03 to 0.3
Outputs:
- grad_qkv: bfloat16 [8, 3, 512, 16, 128], P('dp', None, 'seq')
- d_smooth: float32 [2048], replicated
- d_clip: float32 [3072], replicated
The draws below stay inside these ranges and needn't reach their ends.
All inputs are finite; a program needn't handle non-finite values. Where the reference program divides by a largest or mean magnitude, that divisor is 1e-20 or more.
Results may differ from the reference program's by a relative error of at most 0.03.
Values may be sent and summed in bfloat16 or wider, within the bound.
A program may use at most 64 MiB of HBM per device.

```python
import math
import jax
import jax.numpy as jnp
from jax import lax

D = 3072
HEADS = 16
HEAD_DIM = 128
LEN = 512
VIDEOS = 8


def draw_qkv(key, part):
    base_key = jax.random.fold_in(key, 0)
    drawn = jax.random.truncated_normal(base_key, -4.0, 4.0, (VIDEOS, 3, LEN, HEADS, HEAD_DIM), jnp.float32)
    return drawn.astype(jnp.bfloat16)


def level_of(stream_key, shape, cuts, low, top_value):
    gain, own = 1.0, jax.random.fold_in(stream_key, 6)
    for dim, parts in cuts:
        steps = jnp.exp(jax.random.uniform(jax.random.fold_in(own, dim), (parts,), jnp.float32, low / len(cuts), top_value / len(cuts)))
        gain = gain * jnp.repeat(steps, shape[dim] // parts).reshape([-1 if axis == dim else 1 for axis in range(len(shape))])
    return gain


def scatter_about(own_key, dims, width, most, shards=(), held_as=jnp.bfloat16):
    level = level_of(own_key, dims, shards, -0.22, 0.18) if shards else 1.0
    values = jax.random.normal(own_key, dims, jnp.float32) * width * level
    return jnp.minimum(jnp.maximum(values, -most), most).astype(held_as)


def setup_inputs(seed: int = 0) -> dict:
    seeds = jax.random.split(jax.random.key(seed), 5)
    return {
        "qkv": draw_qkv(jax.random.fold_in(seeds[4], 71), 0),
        "cotangent": scatter_about(seeds[1], (VIDEOS, LEN, D), 1.0, 6.0, ((0, 8), (1, 4))),
        "w_proj": scatter_about(seeds[2], (HEADS * HEAD_DIM, D), (HEADS * HEAD_DIM) ** -0.5, 0.125),
        "clip_levels": jnp.clip(jnp.exp(jax.random.uniform(seeds[3], (D,), jnp.float32, math.log(0.03), math.log(0.3))), 0.03, 0.3),
    }


epsilon = 1e-05
act_fraction = 0.5
highest = lax.Precision.HIGHEST

def softmax_rows(queries, key_rows):
    scaling = HEAD_DIM ** (-0.5)
    scores = jnp.dot(queries, key_rows.T, precision=highest) * scaling
    row_top = lax.optimization_barrier(jnp.max(scores, axis=-1, keepdims=True))
    exponent = jnp.exp(scores - row_top)
    return exponent / lax.optimization_barrier(jnp.sum(exponent, axis=-1, keepdims=True))

def head_forward(triple):
    queries = triple[0].astype(jnp.float32)
    key_rows = triple[1].astype(jnp.float32)
    values = triple[2].astype(jnp.float32)
    weights = softmax_rows(queries, key_rows)
    weights_low = lax.optimization_barrier(weights.astype(jnp.bfloat16)).astype(jnp.float32)
    return jnp.dot(weights_low, values, precision=highest).astype(jnp.bfloat16)

def head_backward(group):
    scaling = HEAD_DIM ** (-0.5)
    queries = group[0].astype(jnp.float32)
    key_rows = group[1].astype(jnp.float32)
    values = group[2].astype(jnp.float32)
    outputs = group[3].astype(jnp.float32)
    cot_rows = group[4].astype(jnp.float32)
    weights = softmax_rows(queries, key_rows)
    weights_low = lax.optimization_barrier(weights.astype(jnp.bfloat16)).astype(jnp.float32)
    grad_weights = jnp.dot(cot_rows, values.T, precision=highest)
    row_delta = lax.optimization_barrier(jnp.sum(cot_rows * outputs, axis=-1, keepdims=True))
    grad_scores = weights * (grad_weights - row_delta)
    grad_scores = lax.optimization_barrier(grad_scores.astype(jnp.bfloat16)).astype(jnp.float32)
    grad_query = (jnp.dot(grad_scores, key_rows, precision=highest) * scaling).astype(jnp.bfloat16)
    grad_key = (jnp.dot(grad_scores.T, queries, precision=highest) * scaling).astype(jnp.bfloat16)
    grad_value = jnp.dot(weights_low.T, cot_rows, precision=highest).astype(jnp.bfloat16)
    return (grad_query, grad_key, grad_value)

def to_items(tensor):
    return tensor.transpose(0, 2, 1, 3).reshape(VIDEOS * HEADS, LEN, HEAD_DIM)

def reference(qkv, cotangent, w_proj, clip_levels):
    queries = to_items(qkv[:, 0])
    key_rows = to_items(qkv[:, 1])
    values = to_items(qkv[:, 2])
    outputs = lax.map(head_forward, (queries, key_rows, values))
    out_tokens = outputs.reshape(VIDEOS, HEADS, LEN, HEAD_DIM).transpose(0, 2, 1, 3)
    out_float = out_tokens.reshape(VIDEOS * LEN, HEADS * HEAD_DIM).astype(jnp.float32)
    act_max = lax.optimization_barrier(jnp.max(jnp.abs(out_float), axis=0))
    weight_float = w_proj.astype(jnp.float32)
    weight_max = lax.optimization_barrier(jnp.max(jnp.abs(weight_float), axis=1))
    smooth = jnp.sqrt((act_max + epsilon) / (weight_max + epsilon))
    act_clip = act_fraction * jnp.max(jnp.sqrt((act_max + epsilon) * (weight_max + epsilon)))
    smoothed = out_float / smooth
    act_tanh = jnp.tanh(smoothed / act_clip)
    act_quant = (act_clip * act_tanh).astype(jnp.bfloat16)
    ratio = smooth[:, None] * weight_float / clip_levels[None, :]
    weight_tanh = jnp.tanh(ratio)
    weight_quant = (clip_levels[None, :] * weight_tanh).astype(jnp.bfloat16)
    cot_rows = cotangent.reshape(VIDEOS * LEN, D).astype(jnp.float32)
    grad_act = jnp.dot(cot_rows, weight_quant.astype(jnp.float32).T, precision=highest)
    grad_weight = jnp.dot(act_quant.astype(jnp.float32).T, cot_rows, precision=highest)
    weight_slope = 1.0 - weight_tanh * weight_tanh
    d_clip = lax.optimization_barrier(jnp.sum(grad_weight * (weight_tanh - ratio * weight_slope), axis=0))
    grad_smoothed = grad_act * (1.0 - act_tanh * act_tanh)
    weight_part = lax.optimization_barrier(jnp.sum(grad_weight * weight_slope * weight_float, axis=1))
    act_part = lax.optimization_barrier(jnp.sum(grad_smoothed * out_float, axis=0)) / (smooth * smooth)
    d_smooth = weight_part - act_part
    grad_out = (grad_smoothed / smooth).astype(jnp.bfloat16)
    cot_items = to_items(grad_out.reshape(VIDEOS, LEN, HEADS, HEAD_DIM))
    grads = lax.map(head_backward, (queries, key_rows, values, outputs, cot_items))
    stacked = jnp.stack(grads, axis=0).reshape(3, VIDEOS, HEADS, LEN, HEAD_DIM)
    grad_qkv = stacked.transpose(1, 0, 3, 2, 4)
    return (grad_qkv, d_smooth, d_clip)
```

```python
import functools

import jax
import jax.numpy as jnp
from jax import lax
from jax.experimental import pallas as pl
from jax.experimental.pallas import tpu as pltpu
from jax.sharding import PartitionSpec as P

epsilon = 1e-05
act_fraction = 0.5
LANES = 128
PAD = 8
EARLY = 3
f32 = jnp.float32
bf16 = jnp.bfloat16


def dot(a, b, da, db):
    return lax.dot_general(a, b, (((da,), (db,)), ((), ())), preferred_element_type=f32)


def remote(src, dst, send, recv, to_seq, to_dp):
    return pltpu.make_async_remote_copy(
        src_ref=src,
        dst_ref=dst,
        send_sem=send,
        recv_sem=recv,
        device_id={"seq": to_seq, "dp": to_dp},
        device_id_type=pl.DeviceIdType.MESH,
    )


def wait_for(ref, sem):
    pltpu.make_async_copy(ref, ref, sem).wait()


def lane(index):
    return pl.ds(pl.multiple_of(index * LANES, LANES), LANES)


def kernel(
    S, N, nh, T, D, CW,
    qkv, cot, w, clip,
    gout, sout, cout,
    hbuf, cbuf, wbuf, pbuf, obuf, tbuf, qbuf, wt, wq, ga, dbuf, gbuf,
    wmax, smooth_ref, scol, wacc, m1, m2, r1, r2,
    w_sem, qsend, qrecv, csend, cback, coth, crecv, gsend, grecv,
    m1s, m1r, m2s, m2r, r1s, r1r, r2s, r2r,
):
    s = lax.axis_index("seq")
    d = lax.axis_index("dp")
    H = S // 2
    p = lax.rem(d, 2)
    h = s // H
    i = lax.rem(s, H)
    base = d - p
    mate = base + 1 - p
    g = 2 * i + p
    chunks = D // CW
    head_dim = LANES
    scaling = head_dim ** (-0.5)
    own_rows = pl.ds(pl.multiple_of(s * T, T), T)
    clip_rows = D // LANES

    barrier = pltpu.get_barrier_semaphore()

    def greet(a, b):
        pl.semaphore_signal(
            barrier, inc=1, device_id={"seq": a, "dp": b}, device_id_type=pl.DeviceIdType.MESH
        )

    for k in range(1, N):
        greet(s, lax.rem(d + k, N))
    for k in range(1, S):
        greet(lax.rem(s + k, S), d)
        greet(lax.rem(s + k, S), mate)
    w_copy = pltpu.make_async_copy(w, wbuf, w_sem)
    w_copy.start()
    pl.semaphore_wait(barrier, N - 1 + 2 * (S - 1))

    def own_cot(c, start):
        cols = pl.ds(pl.multiple_of(c * CW, CW), CW)
        src = cot.at[:, cols]
        dst = cbuf.at[own_rows, cols]

        def go(send, a, b):
            if start:
                remote(src, dst, send, crecv.at[s, c], a, b).start()
            else:
                wait_for(src, send)

        @pl.when(p != h)
        def _():
            go(csend.at[s, c], (H - 1) + p, d)

        @pl.when(p == h)
        def _():
            if start:
                pltpu.make_async_copy(src, dst, crecv.at[s, c]).start()
            go(coth.at[s, c], s, mate)

            @pl.when(i + 1 < H)
            def _():
                go(csend.at[s, c], s + 1, d)

            @pl.when(i > 0)
            def _():
                go(cback.at[c], s - 1, d)

    def forward(c, start):
        cols = pl.ds(pl.multiple_of(c * CW, CW), CW)
        for k in range(S):

            @pl.when(jnp.logical_and(p == h, s != k))
            def _():
                block = cbuf.at[pl.ds(k * T, T), cols]
                if start:
                    wait_for(block, crecv.at[k, c])

                def go(send, a, b):
                    if start:
                        remote(block, block, send, crecv.at[k, c], a, b).start()
                    else:
                        wait_for(block, send)

                @pl.when(jnp.logical_and(s > k, i + 1 < H))
                def _():
                    go(csend.at[k, c], s + 1, d)

                @pl.when(jnp.logical_and(s < k, i > 0))
                def _():
                    go(csend.at[k, c], s - 1, d)

                go(coth.at[k, c], s, mate)

    def await_cot(c):
        cols = pl.ds(pl.multiple_of(c * CW, CW), CW)
        for k in range(S):

            @pl.when(jnp.logical_or(p != h, s == k))
            def _():
                wait_for(cbuf.at[pl.ds(k * T, T), cols], crecv.at[k, c])

    def each(count, body):
        def step(n, carry):
            body(n)
            return carry

        lax.fori_loop(0, count, step, 0)

    def send_heads(n, start):
        hh = n // S
        to = lax.rem(n, S)
        a = p * H + to // 2
        b = base + lax.rem(to, 2)
        mine = jnp.logical_and(a == s, b == d)
        src = qkv.at[:, :, lane(to * nh + hh)]
        dst = hbuf.at[hh, :, own_rows, :]

        @pl.when(mine)
        def _():
            if start:
                pltpu.make_async_copy(src, dst, qrecv.at[hh, s]).start()

        @pl.when(jnp.logical_not(mine))
        def _():
            if start:
                remote(src, dst, qsend.at[hh, to], qrecv.at[hh, s], a, b).start()
            else:
                wait_for(src, qsend.at[hh, to])

    early = min(EARLY, chunks)
    each(early, lambda c: own_cot(c, True))
    each(nh * S, lambda n: send_heads(n, True))
    each(chunks - early, lambda c: own_cot(c + early, True))

    w_copy.wait()
    wmax[...] = jnp.zeros_like(wmax)

    def weight_rows(gg):
        for hh in range(nh):
            rows = pl.ds(pl.multiple_of((gg * nh + hh) * LANES, LANES), LANES)
            top = jnp.zeros((LANES, LANES), f32)
            for t in range(clip_rows):
                top = jnp.maximum(
                    top, jnp.abs(wbuf[rows, t * LANES:(t + 1) * LANES].astype(f32))
                )
            wmax[gg, hh:hh + 1, :] = jnp.max(top.T, axis=0, keepdims=True)

    each(S, weight_rows)
    each(early, lambda c: forward(c, True))

    m1[d] = jnp.zeros((PAD, LANES), f32)
    for hh in range(nh):
        for k in range(S):
            wait_for(hbuf.at[hh, :, pl.ds(k * T, T), :], qrecv.at[hh, k])
        scores = dot(hbuf[hh, 0], hbuf[hh, 1], 1, 1) * scaling
        top = jnp.max(scores, axis=-1, keepdims=True)
        e = jnp.exp(scores - top)
        weights = (e * (1.0 / jnp.sum(e, axis=-1, keepdims=True))).astype(bf16)
        pbuf[hh] = weights
        o = dot(weights, hbuf[hh, 2], 1, 0).astype(bf16)
        obuf[hh] = o
        m1[d, hh:hh + 1, :] = jnp.max(jnp.abs(o.astype(f32)), axis=0, keepdims=True)

    def to_plane(buf, ss, rs, start):
        for k in range(1, N):
            b = lax.rem(d + k, N)
            if start:
                remote(buf.at[d], buf.at[d], ss.at[k], rs.at[d], s, b).start()
            else:
                wait_for(buf.at[d], ss.at[k])

    def from_plane(buf, rs):
        for k in range(1, N):
            b = lax.rem(d + k, N)
            wait_for(buf.at[b], rs.at[b])

    def to_line(buf, ss, rs, start):
        for k in range(1, S):
            a = lax.rem(s + k, S)
            if start:
                remote(buf.at[s], buf.at[s], ss.at[k], rs.at[s], a, d).start()
            else:
                wait_for(buf.at[s], ss.at[k])

    def from_line(buf, rs):
        for k in range(1, S):
            a = lax.rem(s + k, S)
            wait_for(buf.at[a], rs.at[a])

    to_plane(m1, m1s, m1r, True)
    late = chunks - early
    first = (late + 2) // 3
    second = (late - first + 1) // 2
    m2[s] = jnp.zeros((S, PAD, LANES), f32)
    from_plane(m1, m1r)
    for q in range(2):
        m2[s, 2 * i + q] = functools.reduce(jnp.maximum, [m1[k] for k in range(q, N, 2)])
    to_line(m2, m2s, m2r, True)
    each(first, lambda c: forward(c + early, True))
    from_line(m2, m2r)
    act_max = functools.reduce(jnp.maximum, [m2[k] for k in range(S)])
    weight_max = wmax[...]
    smooth_all = jnp.sqrt((act_max + epsilon) / (weight_max + epsilon))
    act_clip = act_fraction * jnp.max(
        jnp.sqrt((act_max + epsilon) * (weight_max + epsilon)), keepdims=True
    ).reshape(1, 1)
    smooth_ref[...] = smooth_all
    own_smooth = smooth_ref[g]

    for hh in range(nh):
        scol[hh] = jnp.broadcast_to(own_smooth[hh:hh + 1, :], (LANES, LANES)).T
    reps = CW // LANES

    def weight_tile(c, hh):
        cols = pl.ds(pl.multiple_of(c * CW, CW), CW)
        rows = pl.ds(pl.multiple_of((g * nh + hh) * LANES, LANES), LANES)
        w_tile = wbuf[rows, cols].astype(f32)
        wide = jnp.concatenate([scol[hh]] * reps, axis=1)
        return w_tile, wide * w_tile / clip[:, cols]

    def weight_chunk(c):
        cols = pl.ds(pl.multiple_of(c * CW, CW), CW)
        for hh in range(nh):
            part = slice(hh * LANES, (hh + 1) * LANES)
            _, ratio = weight_tile(c, hh)
            th = jnp.tanh(ratio)
            wt[part, cols] = th
            wq[part, cols] = (clip[:, cols] * th).astype(bf16)

    each(chunks, weight_chunk)
    each(second, lambda c: forward(c + early + first, True))
    for hh in range(nh):
        part = slice(hh * LANES, (hh + 1) * LANES)
        th = jnp.tanh(obuf[hh].astype(f32) / own_smooth[hh:hh + 1, :] / act_clip)
        tbuf[:, part] = th
        qbuf[:, part] = (act_clip * th).astype(bf16)
    each(late - first - second, lambda c: forward(c + early + first + second, True))

    ga[...] = jnp.zeros_like(ga)

    def grad_chunk(c):
        cols = pl.ds(pl.multiple_of(c * CW, CW), CW)
        await_cot(c)
        ga[...] += dot(cbuf[:, cols], wq[:, cols], 1, 1)

    each(chunks, grad_chunk)

    def send_grads(hh, start):
        for k in range(S):
            b = base + h
            mine = jnp.logical_and(s == k, d == b)
            src = gbuf.at[hh, :, pl.ds(k * T, T), :]
            dst = gout.at[:, :, lane(g * nh + hh)]

            @pl.when(mine)
            def _():
                if start:
                    pltpu.make_async_copy(src, dst, grecv.at[g, hh]).start()

            @pl.when(jnp.logical_not(mine))
            def _():
                if start:
                    remote(src, dst, gsend.at[k, hh], grecv.at[g, hh], k, b).start()
                else:
                    wait_for(src, gsend.at[k, hh])

    act_parts = []
    for hh in range(nh):
        part = slice(hh * LANES, (hh + 1) * LANES)
        sm = own_smooth[hh:hh + 1, :]
        th = tbuf[:, part]
        o = obuf[hh].astype(f32)
        gs = ga[:, part] * (1.0 - th * th)
        act_parts.append(jnp.sum(gs * o, axis=0, keepdims=True) / (sm * sm))
        do = (gs / sm).astype(bf16)
        delta = jnp.sum(do.astype(f32) * o, axis=-1, keepdims=True)
        weights = pbuf[hh]
        ds = (weights.astype(f32) * (dot(do, hbuf[hh, 2], 1, 1) - delta)).astype(bf16)
        gbuf[hh, 0] = (dot(ds, hbuf[hh, 1], 1, 0) * scaling).astype(bf16)
        gbuf[hh, 1] = (dot(ds, hbuf[hh, 0], 0, 0) * scaling).astype(bf16)
        gbuf[hh, 2] = dot(weights, do, 0, 0).astype(bf16)
        send_grads(hh, True)

    wacc[...] = jnp.zeros_like(wacc)

    def clip_chunk(c):
        cols = pl.ds(pl.multiple_of(c * CW, CW), CW)
        gw = dot(qbuf[...], cbuf[:, cols], 0, 0)
        total = jnp.zeros((1, CW), f32)
        for hh in range(nh):
            part = slice(hh * LANES, (hh + 1) * LANES)
            w_tile, ratio = weight_tile(c, hh)
            th = wt[part, cols]
            gpart = gw[part]
            slope = 1.0 - th * th
            total += jnp.sum(gpart * (th - ratio * slope), axis=0, keepdims=True)
            term = gpart * slope * w_tile
            wacc[part] += sum(term[:, t * LANES:(t + 1) * LANES] for t in range(reps))
        for t in range(reps):
            dbuf[pl.ds(c * reps + t, 1), :] = total[:, t * LANES:(t + 1) * LANES]

    each(chunks, clip_chunk)
    r1[d] = jnp.zeros((clip_rows + PAD, LANES), f32)
    r1[d, 0:clip_rows] = dbuf[...]
    for hh in range(nh):
        row = jnp.sum(wacc[hh * LANES:(hh + 1) * LANES].T, axis=0, keepdims=True) - act_parts[hh]
        r1[d, clip_rows + hh:clip_rows + hh + 1, :] = row
    to_plane(r1, r1s, r1r, True)
    from_plane(r1, r1r)
    r2[s] = jnp.zeros((clip_rows + S * PAD, LANES), f32)
    r2[s, 0:clip_rows] = sum(r1[k, 0:clip_rows] for k in range(N))
    for q in range(2):
        at = pl.ds(pl.multiple_of(clip_rows + (2 * i + q) * PAD, PAD), PAD)
        r2[s, at] = sum(r1[k, clip_rows:clip_rows + PAD] for k in range(q, N, 2))
    to_line(r2, r2s, r2r, True)
    from_line(r2, r2r)
    total = sum(r2[k] for k in range(S))
    cout[...] = total[0:clip_rows]
    for gg in range(S):
        at = clip_rows + gg * PAD
        sout[gg * nh:(gg + 1) * nh] = total[at:at + nh]

    for gg in range(S):
        for hh in range(nh):
            wait_for(gout.at[:, :, lane(gg * nh + hh)], grecv.at[gg, hh])
    each(chunks, lambda c: own_cot(c, False))
    each(chunks, lambda c: forward(c, False))
    each(nh * S, lambda n: send_heads(n, False))
    for hh in range(nh):
        send_grads(hh, False)
    to_plane(m1, m1s, m1r, False)
    to_plane(r1, r1s, r1r, False)
    to_line(m2, m2s, m2r, False)
    to_line(r2, r2s, r2r, False)


def per_device(S, N, qkv, cotangent, w_proj, clip_levels):
    _, three, T, heads, head_dim = qkv.shape
    C, D = w_proj.shape
    nh = heads // S
    L = T * S
    CW = D // 6
    cg = nh * head_dim
    chunks = D // CW
    clip_rows = D // LANES
    flat = qkv.reshape(three, T, C)
    vmem = pl.BlockSpec(memory_space=pltpu.VMEM)
    anyspace = pl.BlockSpec(memory_space=pl.ANY)
    dma = pltpu.SemaphoreType.DMA
    gout, sout, cout = pl.pallas_call(
        functools.partial(kernel, S, N, nh, T, D, CW),
        out_shape=(
            jax.ShapeDtypeStruct((three, T, C), bf16),
            jax.ShapeDtypeStruct((heads, LANES), f32),
            jax.ShapeDtypeStruct((clip_rows, LANES), f32),
        ),
        in_specs=[anyspace, anyspace, anyspace, vmem],
        out_specs=(anyspace, vmem, vmem),
        scratch_shapes=[
            pltpu.VMEM((nh, three, L, head_dim), bf16),
            pltpu.VMEM((L, D), bf16),
            pltpu.VMEM((C, D), bf16),
            pltpu.VMEM((nh, L, L), bf16),
            pltpu.VMEM((nh, L, head_dim), bf16),
            pltpu.VMEM((L, cg), f32),
            pltpu.VMEM((L, cg), bf16),
            pltpu.VMEM((cg, D), f32),
            pltpu.VMEM((cg, D), bf16),
            pltpu.VMEM((L, cg), f32),
            pltpu.VMEM((clip_rows, LANES), f32),
            pltpu.VMEM((nh, three, L, head_dim), bf16),
            pltpu.VMEM((S, PAD, LANES), f32),
            pltpu.VMEM((S, PAD, LANES), f32),
            pltpu.VMEM((nh, LANES, LANES), f32),
            pltpu.VMEM((cg, LANES), f32),
            pltpu.VMEM((N, PAD, LANES), f32),
            pltpu.VMEM((S, S, PAD, LANES), f32),
            pltpu.VMEM((N, clip_rows + PAD, LANES), f32),
            pltpu.VMEM((S, clip_rows + S * PAD, LANES), f32),
            dma,
            dma((nh, S)), dma((nh, S)),
            dma((S, chunks)), dma((chunks,)), dma((S, chunks)), dma((S, chunks)),
            dma((S, nh)), dma((S, nh)),
            dma((N,)), dma((N,)), dma((S,)), dma((S,)),
            dma((N,)), dma((N,)), dma((S,)), dma((S,)),
        ],
        compiler_params=pltpu.CompilerParams(
            collective_id=0, has_side_effects=True, vmem_limit_bytes=60000 * 1024
        ),
    )(flat, cotangent[0], w_proj, clip_levels.reshape(1, D))
    return (gout.reshape(qkv.shape), sout.reshape(C), cout.reshape(D))


def solution(mesh):
    in_specs = (P("dp", None, "seq", None, None), P("dp", "seq", None), P(), P())
    out_specs = (P("dp", None, "seq", None, None), P(), P())
    body = functools.partial(per_device, mesh.shape["seq"], mesh.shape["dp"])
    return jax.shard_map(
        body, mesh=mesh, in_specs=in_specs, out_specs=out_specs, check_vma=False
    )
```

```python
import functools

import jax
import jax.numpy as jnp
from jax import lax
from jax.experimental import pallas as pl
from jax.experimental.pallas import tpu as pltpu
from jax.sharding import PartitionSpec as P

epsilon = 1e-05
act_fraction = 0.5
LANES = 128
PAD = 8
EARLY = 3
f32 = jnp.float32
bf16 = jnp.bfloat16


def dot(a, b, da, db):
    return lax.dot_general(a, b, (((da,), (db,)), ((), ())), preferred_element_type=f32)


def remote(src, dst, send, recv, to_seq, to_dp):
    return pltpu.make_async_remote_copy(
        src_ref=src,
        dst_ref=dst,
        send_sem=send,
        recv_sem=recv,
        device_id={"seq": to_seq, "dp": to_dp},
        device_id_type=pl.DeviceIdType.MESH,
    )


def wait_for(ref, sem):
    pltpu.make_async_copy(ref, ref, sem).wait()


def lane(index):
    return pl.ds(pl.multiple_of(index * LANES, LANES), LANES)


def kernel(
    S, N, nh, T, D, CW,
    qkv, cot, w, clip,
    gout, sout, cout,
    xbuf, sbuf, hbuf, cbuf, wbuf, pbuf, obuf, tbuf, qbuf, wt, wq, ga, dbuf, gbuf,
    wmax, smooth_ref, scol, wacc, m1, m2, r1, r2,
    w_sem, x_sem, qsend, qrecv, csend, cback, coth, crecv, gsend, grecv,
    m1s, m1r, m2s, m2r, r1s, r1r, r2s, r2r,
):
    s = lax.axis_index("seq")
    d = lax.axis_index("dp")
    H = S // 2
    p = lax.rem(d, 2)
    h = s // H
    i = lax.rem(s, H)
    base = d - p
    mate = base + 1 - p
    g = 2 * i + p
    chunks = D // CW
    head_dim = LANES
    scaling = head_dim ** (-0.5)
    own_rows = pl.ds(pl.multiple_of(s * T, T), T)
    clip_rows = D // LANES

    barrier = pltpu.get_barrier_semaphore()

    def greet(a, b):
        pl.semaphore_signal(
            barrier, inc=1, device_id={"seq": a, "dp": b}, device_id_type=pl.DeviceIdType.MESH
        )

    for k in range(1, N):
        greet(s, lax.rem(d + k, N))
    for k in range(1, S):
        greet(lax.rem(s + k, S), d)
        greet(lax.rem(s + k, S), mate)
    w_copy = pltpu.make_async_copy(w, wbuf, w_sem)
    x_copy = pltpu.make_async_copy(qkv.at[0], xbuf, x_sem)
    x_copy.start()
    w_copy.start()
    pl.semaphore_wait(barrier, N - 1 + 2 * (S - 1))

    def own_cot(c, start):
        cols = pl.ds(pl.multiple_of(c * CW, CW), CW)
        src = cot.at[:, cols]
        dst = cbuf.at[own_rows, cols]

        def go(send, a, b):
            if start:
                remote(src, dst, send, crecv.at[s, c], a, b).start()
            else:
                wait_for(src, send)

        @pl.when(p != h)
        def _():
            go(csend.at[s, c], (H - 1) + p, d)

        @pl.when(p == h)
        def _():
            if start:
                pltpu.make_async_copy(src, dst, crecv.at[s, c]).start()
            go(coth.at[s, c], s, mate)

            @pl.when(i + 1 < H)
            def _():
                go(csend.at[s, c], s + 1, d)

            @pl.when(i > 0)
            def _():
                go(cback.at[c], s - 1, d)

    def forward(c, start):
        cols = pl.ds(pl.multiple_of(c * CW, CW), CW)
        for k in range(S):

            @pl.when(jnp.logical_and(p == h, s != k))
            def _():
                block = cbuf.at[pl.ds(k * T, T), cols]
                if start:
                    wait_for(block, crecv.at[k, c])

                def go(send, a, b):
                    if start:
                        remote(block, block, send, crecv.at[k, c], a, b).start()
                    else:
                        wait_for(block, send)

                @pl.when(jnp.logical_and(s > k, i + 1 < H))
                def _():
                    go(csend.at[k, c], s + 1, d)

                @pl.when(jnp.logical_and(s < k, i > 0))
                def _():
                    go(csend.at[k, c], s - 1, d)

                go(coth.at[k, c], s, mate)

    def await_cot(c):
        cols = pl.ds(pl.multiple_of(c * CW, CW), CW)
        for k in range(S):

            @pl.when(jnp.logical_or(p != h, s == k))
            def _():
                wait_for(cbuf.at[pl.ds(k * T, T), cols], crecv.at[k, c])

    def each(count, body):
        def step(n, carry):
            body(n)
            return carry

        lax.fori_loop(0, count, step, 0)

    def send_heads(n, start):
        hh = n // S
        to = lax.rem(n, S)
        a = p * H + to // 2
        b = base + lax.rem(to, 2)
        mine = jnp.logical_and(a == s, b == d)
        src = sbuf.at[to * nh + hh]
        dst = hbuf.at[hh, :, own_rows, :]

        @pl.when(mine)
        def _():
            if start:
                pltpu.make_async_copy(src, dst, qrecv.at[hh, s]).start()

        @pl.when(jnp.logical_not(mine))
        def _():
            if start:
                remote(src, dst, qsend.at[hh, to], qrecv.at[hh, s], a, b).start()
            else:
                wait_for(src, qsend.at[hh, to])

    early = min(EARLY, chunks)
    each(early, lambda c: own_cot(c, True))
    x_copy.wait()
    for kk in range(xbuf.shape[0]):
        sbuf[:, kk] = jnp.swapaxes(xbuf[kk], 0, 1)
    each(nh * S, lambda n: send_heads(n, True))
    each(chunks - early, lambda c: own_cot(c + early, True))

    w_copy.wait()
    wmax[...] = jnp.zeros_like(wmax)

    def weight_rows(gg):
        for hh in range(nh):
            rows = pl.ds(pl.multiple_of((gg * nh + hh) * LANES, LANES), LANES)
            top = jnp.zeros((LANES, LANES), f32)
            for t in range(clip_rows):
                top = jnp.maximum(
                    top, jnp.abs(wbuf[rows, t * LANES:(t + 1) * LANES].astype(f32))
                )
            wmax[gg, hh:hh + 1, :] = jnp.max(top.T, axis=0, keepdims=True)

    each(S, weight_rows)
    each(early, lambda c: forward(c, True))

    m1[d] = jnp.zeros((PAD, LANES), f32)
    for hh in range(nh):
        for k in range(S):
            wait_for(hbuf.at[hh, :, pl.ds(k * T, T), :], qrecv.at[hh, k])
        scores = dot(hbuf[hh, 0], hbuf[hh, 1], 1, 1) * scaling
        top = jnp.max(scores, axis=-1, keepdims=True)
        e = jnp.exp(scores - top)
        weights = (e * (1.0 / jnp.sum(e, axis=-1, keepdims=True))).astype(bf16)
        pbuf[hh] = weights
        o = dot(weights, hbuf[hh, 2], 1, 0).astype(bf16)
        obuf[hh] = o
        m1[d, hh:hh + 1, :] = jnp.max(jnp.abs(o.astype(f32)), axis=0, keepdims=True)

    def to_plane(buf, ss, rs, start):
        for k in range(1, N):
            b = lax.rem(d + k, N)
            if start:
                remote(buf.at[d], buf.at[d], ss.at[k], rs.at[d], s, b).start()
            else:
                wait_for(buf.at[d], ss.at[k])

    def from_plane(buf, rs):
        for k in range(1, N):
            b = lax.rem(d + k, N)
            wait_for(buf.at[b], rs.at[b])

    def to_line(buf, ss, rs, start):
        for k in range(1, S):
            a = lax.rem(s + k, S)
            if start:
                remote(buf.at[s], buf.at[s], ss.at[k], rs.at[s], a, d).start()
            else:
                wait_for(buf.at[s], ss.at[k])

    def from_line(buf, rs):
        for k in range(1, S):
            a = lax.rem(s + k, S)
            wait_for(buf.at[a], rs.at[a])

    to_plane(m1, m1s, m1r, True)
    late = chunks - early
    first = (late + 2) // 3
    second = (late - first + 1) // 2
    m2[s] = jnp.zeros((S, PAD, LANES), f32)
    from_plane(m1, m1r)
    for q in range(2):
        m2[s, 2 * i + q] = functools.reduce(jnp.maximum, [m1[k] for k in range(q, N, 2)])
    to_line(m2, m2s, m2r, True)
    each(first, lambda c: forward(c + early, True))
    from_line(m2, m2r)
    act_max = functools.reduce(jnp.maximum, [m2[k] for k in range(S)])
    weight_max = wmax[...]
    smooth_all = jnp.sqrt((act_max + epsilon) / (weight_max + epsilon))
    act_clip = act_fraction * jnp.max(
        jnp.sqrt((act_max + epsilon) * (weight_max + epsilon)), keepdims=True
    ).reshape(1, 1)
    smooth_ref[...] = smooth_all
    own_smooth = smooth_ref[g]

    for hh in range(nh):
        scol[hh] = jnp.broadcast_to(own_smooth[hh:hh + 1, :], (LANES, LANES)).T
    reps = CW // LANES

    def weight_tile(c, hh):
        cols = pl.ds(pl.multiple_of(c * CW, CW), CW)
        rows = pl.ds(pl.multiple_of((g * nh + hh) * LANES, LANES), LANES)
        w_tile = wbuf[rows, cols].astype(f32)
        wide = jnp.concatenate([scol[hh]] * reps, axis=1)
        return w_tile, wide * w_tile / clip[:, cols]

    def weight_chunk(c):
        cols = pl.ds(pl.multiple_of(c * CW, CW), CW)
        for hh in range(nh):
            part = slice(hh * LANES, (hh + 1) * LANES)
            _, ratio = weight_tile(c, hh)
            th = jnp.tanh(ratio)
            wt[part, cols] = th
            wq[part, cols] = (clip[:, cols] * th).astype(bf16)

    each(chunks, weight_chunk)
    each(second, lambda c: forward(c + early + first, True))
    for hh in range(nh):
        part = slice(hh * LANES, (hh + 1) * LANES)
        th = jnp.tanh(obuf[hh].astype(f32) / own_smooth[hh:hh + 1, :] / act_clip)
        tbuf[:, part] = th
        qbuf[:, part] = (act_clip * th).astype(bf16)

    ga[...] = jnp.zeros_like(ga)

    def grad_chunk(c):
        cols = pl.ds(pl.multiple_of(c * CW, CW), CW)
        await_cot(c)
        ga[...] += dot(cbuf[:, cols], wq[:, cols], 1, 1)

    ready = early + first + second

    def late_chunk(n):
        forward(n + ready, True)
        grad_chunk(n + ready)

    each(ready, grad_chunk)
    each(chunks - ready, late_chunk)

    def send_grads(hh, start):
        for n in range(S):
            k = h * n + (1 - h) * (S - 1 - n)
            b = base + h
            mine = jnp.logical_and(s == k, d == b)
            src = gbuf.at[hh, :, pl.ds(pl.multiple_of(k * T, T), T), :]
            dst = gout.at[:, :, lane(g * nh + hh)]

            @pl.when(mine)
            def _():
                if start:
                    pltpu.make_async_copy(src, dst, grecv.at[g, hh]).start()

            @pl.when(jnp.logical_not(mine))
            def _():
                if start:
                    remote(src, dst, gsend.at[k, hh], grecv.at[g, hh], k, b).start()
                else:
                    wait_for(src, gsend.at[k, hh])

    act_parts = []
    for hh in range(nh):
        part = slice(hh * LANES, (hh + 1) * LANES)
        sm = own_smooth[hh:hh + 1, :]
        th = tbuf[:, part]
        o = obuf[hh].astype(f32)
        gs = ga[:, part] * (1.0 - th * th)
        act_parts.append(jnp.sum(gs * o, axis=0, keepdims=True) / (sm * sm))
        do = (gs / sm).astype(bf16)
        delta = jnp.sum(do.astype(f32) * o, axis=-1, keepdims=True)
        weights = pbuf[hh]
        ds = (weights.astype(f32) * (dot(do, hbuf[hh, 2], 1, 1) - delta)).astype(bf16)
        gbuf[hh, 0] = (dot(ds, hbuf[hh, 1], 1, 0) * scaling).astype(bf16)
        gbuf[hh, 1] = (dot(ds, hbuf[hh, 0], 0, 0) * scaling).astype(bf16)
        gbuf[hh, 2] = dot(weights, do, 0, 0).astype(bf16)
        send_grads(hh, True)

    wacc[...] = jnp.zeros_like(wacc)

    def clip_chunk(c):
        cols = pl.ds(pl.multiple_of(c * CW, CW), CW)
        gw = dot(qbuf[...], cbuf[:, cols], 0, 0)
        total = jnp.zeros((1, CW), f32)
        for hh in range(nh):
            part = slice(hh * LANES, (hh + 1) * LANES)
            w_tile, ratio = weight_tile(c, hh)
            th = wt[part, cols]
            gpart = gw[part]
            slope = 1.0 - th * th
            total += jnp.sum(gpart * (th - ratio * slope), axis=0, keepdims=True)
            term = gpart * slope * w_tile
            wacc[part] += sum(term[:, t * LANES:(t + 1) * LANES] for t in range(reps))
        for t in range(reps):
            dbuf[pl.ds(c * reps + t, 1), :] = total[:, t * LANES:(t + 1) * LANES]

    each(chunks, clip_chunk)
    r1[d] = jnp.zeros((clip_rows + PAD, LANES), f32)
    r1[d, 0:clip_rows] = dbuf[...]
    for hh in range(nh):
        row = jnp.sum(wacc[hh * LANES:(hh + 1) * LANES].T, axis=0, keepdims=True) - act_parts[hh]
        r1[d, clip_rows + hh:clip_rows + hh + 1, :] = row
    to_plane(r1, r1s, r1r, True)
    from_plane(r1, r1r)
    r2[s] = jnp.zeros((clip_rows + S * PAD, LANES), f32)
    r2[s, 0:clip_rows] = sum(r1[k, 0:clip_rows] for k in range(N))
    for q in range(2):
        at = pl.ds(pl.multiple_of(clip_rows + (2 * i + q) * PAD, PAD), PAD)
        r2[s, at] = sum(r1[k, clip_rows:clip_rows + PAD] for k in range(q, N, 2))
    to_line(r2, r2s, r2r, True)
    from_line(r2, r2r)
    total = sum(r2[k] for k in range(S))
    cout[...] = total[0:clip_rows]
    for gg in range(S):
        at = clip_rows + gg * PAD
        sout[gg * nh:(gg + 1) * nh] = total[at:at + nh]

    for gg in range(S):
        for hh in range(nh):
            wait_for(gout.at[:, :, lane(gg * nh + hh)], grecv.at[gg, hh])
    each(chunks, lambda c: own_cot(c, False))
    each(chunks, lambda c: forward(c, False))
    each(nh * S, lambda n: send_heads(n, False))
    for hh in range(nh):
        send_grads(hh, False)
    to_plane(m1, m1s, m1r, False)
    to_plane(r1, r1s, r1r, False)
    to_line(m2, m2s, m2r, False)
    to_line(r2, r2s, r2r, False)


def per_device(S, N, qkv, cotangent, w_proj, clip_levels):
    _, three, T, heads, head_dim = qkv.shape
    C, D = w_proj.shape
    nh = heads // S
    L = T * S
    CW = D // 6
    cg = nh * head_dim
    chunks = D // CW
    clip_rows = D // LANES
    vmem = pl.BlockSpec(memory_space=pltpu.VMEM)
    anyspace = pl.BlockSpec(memory_space=pl.ANY)
    dma = pltpu.SemaphoreType.DMA
    gout, sout, cout = pl.pallas_call(
        functools.partial(kernel, S, N, nh, T, D, CW),
        out_shape=(
            jax.ShapeDtypeStruct((three, T, C), bf16),
            jax.ShapeDtypeStruct((heads, LANES), f32),
            jax.ShapeDtypeStruct((clip_rows, LANES), f32),
        ),
        in_specs=[anyspace, anyspace, anyspace, vmem],
        out_specs=(anyspace, vmem, vmem),
        scratch_shapes=[
            pltpu.VMEM((three, T, heads, head_dim), bf16),
            pltpu.VMEM((heads, three, T, head_dim), bf16),
            pltpu.VMEM((nh, three, L, head_dim), bf16),
            pltpu.VMEM((L, D), bf16),
            pltpu.VMEM((C, D), bf16),
            pltpu.VMEM((nh, L, L), bf16),
            pltpu.VMEM((nh, L, head_dim), bf16),
            pltpu.VMEM((L, cg), f32),
            pltpu.VMEM((L, cg), bf16),
            pltpu.VMEM((cg, D), f32),
            pltpu.VMEM((cg, D), bf16),
            pltpu.VMEM((L, cg), f32),
            pltpu.VMEM((clip_rows, LANES), f32),
            pltpu.VMEM((nh, three, L, head_dim), bf16),
            pltpu.VMEM((S, PAD, LANES), f32),
            pltpu.VMEM((S, PAD, LANES), f32),
            pltpu.VMEM((nh, LANES, LANES), f32),
            pltpu.VMEM((cg, LANES), f32),
            pltpu.VMEM((N, PAD, LANES), f32),
            pltpu.VMEM((S, S, PAD, LANES), f32),
            pltpu.VMEM((N, clip_rows + PAD, LANES), f32),
            pltpu.VMEM((S, clip_rows + S * PAD, LANES), f32),
            dma,
            dma,
            dma((nh, S)), dma((nh, S)),
            dma((S, chunks)), dma((chunks,)), dma((S, chunks)), dma((S, chunks)),
            dma((S, nh)), dma((S, nh)),
            dma((N,)), dma((N,)), dma((S,)), dma((S,)),
            dma((N,)), dma((N,)), dma((S,)), dma((S,)),
        ],
        compiler_params=pltpu.CompilerParams(
            collective_id=0, has_side_effects=True, vmem_limit_bytes=60000 * 1024
        ),
    )(qkv, cotangent[0], w_proj, clip_levels.reshape(1, D))
    return (gout.reshape(qkv.shape), sout.reshape(C), cout.reshape(D))


def solution(mesh):
    in_specs = (P("dp", None, "seq", None, None), P("dp", "seq", None), P(), P())
    out_specs = (P("dp", None, "seq", None, None), P(), P())
    body = functools.partial(per_device, mesh.shape["seq"], mesh.shape["dp"])
    return jax.shard_map(
        body, mesh=mesh, in_specs=in_specs, out_specs=out_specs, check_vma=False
    )
```

```python
import functools

import jax
import jax.numpy as jnp
from jax import lax
from jax.experimental import pallas as pl
from jax.experimental.pallas import tpu as pltpu
from jax.sharding import PartitionSpec as P

epsilon = 1e-05
act_fraction = 0.5
LANES = 128
PAD = 8
EARLY = 3
f32 = jnp.float32
bf16 = jnp.bfloat16


def dot(a, b, da, db):
    return lax.dot_general(a, b, (((da,), (db,)), ((), ())), preferred_element_type=f32)


def remote(src, dst, send, recv, to_seq, to_dp):
    return pltpu.make_async_remote_copy(
        src_ref=src,
        dst_ref=dst,
        send_sem=send,
        recv_sem=recv,
        device_id={"seq": to_seq, "dp": to_dp},
        device_id_type=pl.DeviceIdType.MESH,
    )


def wait_for(ref, sem):
    pltpu.make_async_copy(ref, ref, sem).wait()


def lane(index):
    return pl.ds(pl.multiple_of(index * LANES, LANES), LANES)


def kernel(
    S, N, nh, T, D, CW,
    qkv, cot, w, clip,
    gout, sout, cout,
    xbuf, sbuf, hbuf, cbuf, wbuf, pbuf, obuf, tbuf, qbuf, wt, wq, ga, dbuf, gbuf,
    wmax, smooth_ref, scol, wacc, m1, m2, r1, r2,
    w_sem, x_sem, qsend, qrecv, csend, cback, coth, crecv, gsend, grecv,
    m1s, m1r, m2s, m2r, r1s, r1r, r2s, r2r,
):
    s = lax.axis_index("seq")
    d = lax.axis_index("dp")
    H = S // 2
    p = lax.rem(d, 2)
    h = s // H
    i = lax.rem(s, H)
    base = d - p
    mate = base + 1 - p
    g = 2 * i + p
    chunks = D // CW
    head_dim = LANES
    scaling = head_dim ** (-0.5)
    own_rows = pl.ds(pl.multiple_of(s * T, T), T)
    clip_rows = D // LANES

    barrier = pltpu.get_barrier_semaphore()

    def greet(a, b):
        pl.semaphore_signal(
            barrier, inc=1, device_id={"seq": a, "dp": b}, device_id_type=pl.DeviceIdType.MESH
        )

    for k in range(1, N):
        greet(s, lax.rem(d + k, N))
    for k in range(1, S):
        greet(lax.rem(s + k, S), d)
        greet(lax.rem(s + k, S), mate)
    w_copy = pltpu.make_async_copy(w, wbuf, w_sem)
    x_copy = pltpu.make_async_copy(qkv.at[0], xbuf, x_sem)
    x_copy.start()
    w_copy.start()
    pl.semaphore_wait(barrier, N - 1 + 2 * (S - 1))

    def own_cot(c, start):
        cols = pl.ds(pl.multiple_of(c * CW, CW), CW)
        src = cot.at[:, cols]
        dst = cbuf.at[own_rows, cols]

        def go(send, a, b):
            if start:
                remote(src, dst, send, crecv.at[s, c], a, b).start()
            else:
                wait_for(src, send)

        @pl.when(p != h)
        def _():
            go(csend.at[s, c], (H - 1) + p, d)

        @pl.when(p == h)
        def _():
            if start:
                pltpu.make_async_copy(src, dst, crecv.at[s, c]).start()
            go(coth.at[s, c], s, mate)

            @pl.when(i + 1 < H)
            def _():
                go(csend.at[s, c], s + 1, d)

            @pl.when(i > 0)
            def _():
                go(cback.at[c], s - 1, d)

    def forward(c, start):
        cols = pl.ds(pl.multiple_of(c * CW, CW), CW)
        for k in range(S):

            @pl.when(jnp.logical_and(p == h, s != k))
            def _():
                block = cbuf.at[pl.ds(k * T, T), cols]
                if start:
                    wait_for(block, crecv.at[k, c])

                def go(send, a, b):
                    if start:
                        remote(block, block, send, crecv.at[k, c], a, b).start()
                    else:
                        wait_for(block, send)

                @pl.when(jnp.logical_and(s > k, i + 1 < H))
                def _():
                    go(csend.at[k, c], s + 1, d)

                @pl.when(jnp.logical_and(s < k, i > 0))
                def _():
                    go(csend.at[k, c], s - 1, d)

                go(coth.at[k, c], s, mate)

    def await_cot(c):
        cols = pl.ds(pl.multiple_of(c * CW, CW), CW)
        for k in range(S):

            @pl.when(jnp.logical_or(p != h, s == k))
            def _():
                wait_for(cbuf.at[pl.ds(k * T, T), cols], crecv.at[k, c])

    def each(count, body):
        def step(n, carry):
            body(n)
            return carry

        lax.fori_loop(0, count, step, 0)

    def send_heads(n, start):
        hh = n // S
        to = lax.rem(n, S)
        a = p * H + to // 2
        b = base + lax.rem(to, 2)
        mine = jnp.logical_and(a == s, b == d)
        src = sbuf.at[to * nh + hh]
        dst = hbuf.at[hh, :, own_rows, :]

        @pl.when(mine)
        def _():
            if start:
                pltpu.make_async_copy(src, dst, qrecv.at[hh, s]).start()

        @pl.when(jnp.logical_not(mine))
        def _():
            if start:
                remote(src, dst, qsend.at[hh, to], qrecv.at[hh, s], a, b).start()
            else:
                wait_for(src, qsend.at[hh, to])

    early = min(EARLY, chunks)
    each(early, lambda c: own_cot(c, True))
    x_copy.wait()
    for kk in range(xbuf.shape[0]):
        sbuf[:, kk] = jnp.swapaxes(xbuf[kk], 0, 1)
    each(nh * S, lambda n: send_heads(n, True))
    each(chunks - early, lambda c: own_cot(c + early, True))

    w_copy.wait()
    wmax[...] = jnp.zeros_like(wmax)

    def weight_rows(gg):
        for hh in range(nh):
            rows = pl.ds(pl.multiple_of((gg * nh + hh) * LANES, LANES), LANES)
            top = jnp.zeros((LANES, LANES), f32)
            for t in range(clip_rows):
                top = jnp.maximum(
                    top, jnp.abs(wbuf[rows, t * LANES:(t + 1) * LANES].astype(f32))
                )
            wmax[gg, hh:hh + 1, :] = jnp.max(top.T, axis=0, keepdims=True)

    each(S, weight_rows)
    each(early, lambda c: forward(c, True))

    m1[d] = jnp.zeros((PAD, LANES), f32)
    for hh in range(nh):
        for k in range(S):
            wait_for(hbuf.at[hh, :, pl.ds(k * T, T), :], qrecv.at[hh, k])
        scores = dot(hbuf[hh, 0], hbuf[hh, 1], 1, 1) * scaling
        top = jnp.max(scores, axis=-1, keepdims=True)
        e = jnp.exp(scores - top)
        weights = (e * (1.0 / jnp.sum(e, axis=-1, keepdims=True))).astype(bf16)
        pbuf[hh] = weights
        o = dot(weights, hbuf[hh, 2], 1, 0).astype(bf16)
        obuf[hh] = o
        m1[d, hh:hh + 1, :] = jnp.max(jnp.abs(o.astype(f32)), axis=0, keepdims=True)

    def to_plane(buf, ss, rs, start):
        for k in range(1, N):
            b = lax.rem(d + k, N)
            if start:
                remote(buf.at[d], buf.at[d], ss.at[k], rs.at[d], s, b).start()
            else:
                wait_for(buf.at[d], ss.at[k])

    def from_plane(buf, rs):
        for k in range(1, N):
            b = lax.rem(d + k, N)
            wait_for(buf.at[b], rs.at[b])

    def to_line(buf, ss, rs, start):
        for k in range(1, S):
            a = lax.rem(s + k, S)
            if start:
                remote(buf.at[s], buf.at[s], ss.at[k], rs.at[s], a, d).start()
            else:
                wait_for(buf.at[s], ss.at[k])

    def to_line_idle(start):
        for k in range(1, S):
            a = lax.rem(s + k, S)
            inside = a // H == h
            sender = inside != (p == h)

            @pl.when(sender)
            def _():
                for q, b in enumerate((d, mate)):
                    if start:
                        remote(m2.at[s], m2.at[s], m2s.at[q, k], m2r.at[s], a, b).start()
                    else:
                        wait_for(m2.at[s], m2s.at[q, k])

    def from_line(buf, rs):
        for k in range(1, S):
            a = lax.rem(s + k, S)
            wait_for(buf.at[a], rs.at[a])

    to_plane(m1, m1s, m1r, True)
    late = chunks - early
    first = late
    second = 0
    m2[s] = jnp.zeros((S, PAD, LANES), f32)
    from_plane(m1, m1r)
    for q in range(2):
        m2[s, 2 * i + q] = functools.reduce(jnp.maximum, [m1[k] for k in range(q, N, 2)])
    to_line_idle(True)
    each(first, lambda c: forward(c + early, True))
    from_line(m2, m2r)
    act_max = functools.reduce(jnp.maximum, [m2[k] for k in range(S)])
    weight_max = wmax[...]
    smooth_all = jnp.sqrt((act_max + epsilon) / (weight_max + epsilon))
    act_clip = act_fraction * jnp.max(
        jnp.sqrt((act_max + epsilon) * (weight_max + epsilon)), keepdims=True
    ).reshape(1, 1)
    smooth_ref[...] = smooth_all
    own_smooth = smooth_ref[g]

    for hh in range(nh):
        scol[hh] = jnp.broadcast_to(own_smooth[hh:hh + 1, :], (LANES, LANES)).T
    reps = CW // LANES

    def weight_tile(c, hh):
        cols = pl.ds(pl.multiple_of(c * CW, CW), CW)
        rows = pl.ds(pl.multiple_of((g * nh + hh) * LANES, LANES), LANES)
        w_tile = wbuf[rows, cols].astype(f32)
        wide = jnp.concatenate([scol[hh]] * reps, axis=1)
        return w_tile, wide * w_tile / clip[:, cols]

    def weight_chunk(c):
        cols = pl.ds(pl.multiple_of(c * CW, CW), CW)
        for hh in range(nh):
            part = slice(hh * LANES, (hh + 1) * LANES)
            _, ratio = weight_tile(c, hh)
            th = jnp.tanh(ratio)
            wt[part, cols] = th
            wq[part, cols] = (clip[:, cols] * th).astype(bf16)

    each(chunks, weight_chunk)
    for hh in range(nh):
        part = slice(hh * LANES, (hh + 1) * LANES)
        th = jnp.tanh(obuf[hh].astype(f32) / own_smooth[hh:hh + 1, :] / act_clip)
        tbuf[:, part] = th
        qbuf[:, part] = (act_clip * th).astype(bf16)

    ga[...] = jnp.zeros_like(ga)

    def grad_chunk(c):
        cols = pl.ds(pl.multiple_of(c * CW, CW), CW)
        await_cot(c)
        ga[...] += dot(cbuf[:, cols], wq[:, cols], 1, 1)

    ready = early + first + second

    def late_chunk(n):
        forward(n + ready, True)
        grad_chunk(n + ready)

    each(ready, grad_chunk)
    each(chunks - ready, late_chunk)

    def send_grads(hh, start):
        for n in range(S):
            k = h * n + (1 - h) * (S - 1 - n)
            b = base + h
            mine = jnp.logical_and(s == k, d == b)
            src = gbuf.at[hh, :, pl.ds(pl.multiple_of(k * T, T), T), :]
            dst = gout.at[:, :, lane(g * nh + hh)]

            @pl.when(mine)
            def _():
                if start:
                    pltpu.make_async_copy(src, dst, grecv.at[g, hh]).start()

            @pl.when(jnp.logical_not(mine))
            def _():
                if start:
                    remote(src, dst, gsend.at[k, hh], grecv.at[g, hh], k, b).start()
                else:
                    wait_for(src, gsend.at[k, hh])

    act_parts = []
    for hh in range(nh):
        part = slice(hh * LANES, (hh + 1) * LANES)
        sm = own_smooth[hh:hh + 1, :]
        th = tbuf[:, part]
        o = obuf[hh].astype(f32)
        gs = ga[:, part] * (1.0 - th * th)
        act_parts.append(jnp.sum(gs * o, axis=0, keepdims=True) / (sm * sm))
        do = (gs / sm).astype(bf16)
        delta = jnp.sum(do.astype(f32) * o, axis=-1, keepdims=True)
        weights = pbuf[hh]
        ds = (weights.astype(f32) * (dot(do, hbuf[hh, 2], 1, 1) - delta)).astype(bf16)
        gbuf[hh, 0] = (dot(ds, hbuf[hh, 1], 1, 0) * scaling).astype(bf16)
        gbuf[hh, 1] = (dot(ds, hbuf[hh, 0], 0, 0) * scaling).astype(bf16)
        gbuf[hh, 2] = dot(weights, do, 0, 0).astype(bf16)
        send_grads(hh, True)

    wacc[...] = jnp.zeros_like(wacc)

    def clip_chunk(c):
        cols = pl.ds(pl.multiple_of(c * CW, CW), CW)
        gw = dot(qbuf[...], cbuf[:, cols], 0, 0)
        total = jnp.zeros((1, CW), f32)
        for hh in range(nh):
            part = slice(hh * LANES, (hh + 1) * LANES)
            w_tile, ratio = weight_tile(c, hh)
            th = wt[part, cols]
            gpart = gw[part]
            slope = 1.0 - th * th
            total += jnp.sum(gpart * (th - ratio * slope), axis=0, keepdims=True)
            term = gpart * slope * w_tile
            wacc[part] += sum(term[:, t * LANES:(t + 1) * LANES] for t in range(reps))
        for t in range(reps):
            dbuf[pl.ds(c * reps + t, 1), :] = total[:, t * LANES:(t + 1) * LANES]

    each(chunks, clip_chunk)
    r1[d] = jnp.zeros((clip_rows + PAD, LANES), f32)
    r1[d, 0:clip_rows] = dbuf[...]
    for hh in range(nh):
        row = jnp.sum(wacc[hh * LANES:(hh + 1) * LANES].T, axis=0, keepdims=True) - act_parts[hh]
        r1[d, clip_rows + hh:clip_rows + hh + 1, :] = row
    to_plane(r1, r1s, r1r, True)
    from_plane(r1, r1r)
    r2[s] = jnp.zeros((clip_rows + S * PAD, LANES), f32)
    r2[s, 0:clip_rows] = sum(r1[k, 0:clip_rows] for k in range(N))
    for q in range(2):
        at = pl.ds(pl.multiple_of(clip_rows + (2 * i + q) * PAD, PAD), PAD)
        r2[s, at] = sum(r1[k, clip_rows:clip_rows + PAD] for k in range(q, N, 2))
    to_line(r2, r2s, r2r, True)
    from_line(r2, r2r)
    total = sum(r2[k] for k in range(S))
    cout[...] = total[0:clip_rows]
    for gg in range(S):
        at = clip_rows + gg * PAD
        sout[gg * nh:(gg + 1) * nh] = total[at:at + nh]

    for gg in range(S):
        for hh in range(nh):
            wait_for(gout.at[:, :, lane(gg * nh + hh)], grecv.at[gg, hh])
    each(chunks, lambda c: own_cot(c, False))
    each(chunks, lambda c: forward(c, False))
    each(nh * S, lambda n: send_heads(n, False))
    for hh in range(nh):
        send_grads(hh, False)
    to_plane(m1, m1s, m1r, False)
    to_plane(r1, r1s, r1r, False)
    to_line_idle(False)
    to_line(r2, r2s, r2r, False)


def per_device(S, N, qkv, cotangent, w_proj, clip_levels):
    _, three, T, heads, head_dim = qkv.shape
    C, D = w_proj.shape
    nh = heads // S
    L = T * S
    CW = D // 6
    cg = nh * head_dim
    chunks = D // CW
    clip_rows = D // LANES
    vmem = pl.BlockSpec(memory_space=pltpu.VMEM)
    anyspace = pl.BlockSpec(memory_space=pl.ANY)
    dma = pltpu.SemaphoreType.DMA
    gout, sout, cout = pl.pallas_call(
        functools.partial(kernel, S, N, nh, T, D, CW),
        out_shape=(
            jax.ShapeDtypeStruct((three, T, C), bf16),
            jax.ShapeDtypeStruct((heads, LANES), f32),
            jax.ShapeDtypeStruct((clip_rows, LANES), f32),
        ),
        in_specs=[anyspace, anyspace, anyspace, vmem],
        out_specs=(anyspace, vmem, vmem),
        scratch_shapes=[
            pltpu.VMEM((three, T, heads, head_dim), bf16),
            pltpu.VMEM((heads, three, T, head_dim), bf16),
            pltpu.VMEM((nh, three, L, head_dim), bf16),
            pltpu.VMEM((L, D), bf16),
            pltpu.VMEM((C, D), bf16),
            pltpu.VMEM((nh, L, L), bf16),
            pltpu.VMEM((nh, L, head_dim), bf16),
            pltpu.VMEM((L, cg), f32),
            pltpu.VMEM((L, cg), bf16),
            pltpu.VMEM((cg, D), f32),
            pltpu.VMEM((cg, D), bf16),
            pltpu.VMEM((L, cg), f32),
            pltpu.VMEM((clip_rows, LANES), f32),
            pltpu.VMEM((nh, three, L, head_dim), bf16),
            pltpu.VMEM((S, PAD, LANES), f32),
            pltpu.VMEM((S, PAD, LANES), f32),
            pltpu.VMEM((nh, LANES, LANES), f32),
            pltpu.VMEM((cg, LANES), f32),
            pltpu.VMEM((N, PAD, LANES), f32),
            pltpu.VMEM((S, S, PAD, LANES), f32),
            pltpu.VMEM((N, clip_rows + PAD, LANES), f32),
            pltpu.VMEM((S, clip_rows + S * PAD, LANES), f32),
            dma,
            dma,
            dma((nh, S)), dma((nh, S)),
            dma((S, chunks)), dma((chunks,)), dma((S, chunks)), dma((S, chunks)),
            dma((S, nh)), dma((S, nh)),
            dma((N,)), dma((N,)), dma((2, S)), dma((S,)),
            dma((N,)), dma((N,)), dma((S,)), dma((S,)),
        ],
        compiler_params=pltpu.CompilerParams(
            collective_id=0, has_side_effects=True, vmem_limit_bytes=60000 * 1024
        ),
    )(qkv, cotangent[0], w_proj, clip_levels.reshape(1, D))
    return (gout.reshape(qkv.shape), sout.reshape(C), cout.reshape(D))


def solution(mesh):
    in_specs = (P("dp", None, "seq", None, None), P("dp", "seq", None), P(), P())
    out_specs = (P("dp", None, "seq", None, None), P(), P())
    body = functools.partial(per_device, mesh.shape["seq"], mesh.shape["dp"])
    return jax.shard_map(
        body, mesh=mesh, in_specs=in_specs, out_specs=out_specs, check_vma=False
    )
```
